32 devices in a mesh: seq: 8 (over z, x), head: 4 (over y, core), batch: 1.
Axes of the slice: x: 2, y: 2, z: 4, core: 2. Of those that a mesh axis runs over, the one named last changes fastest.
Arguments:
- queries: bfloat16 [2048, 4096], P(('batch', 'seq', 'head')), may hold values from -6 to 6
- keys: bfloat16 [2048, 512], P(('batch', 'seq', 'head')), may hold values from -6 to 6
- values: bfloat16 [2048, 512], P(('batch', 'seq', 'head')), may hold values from -6 to 6
- page_of_block: int32 [4], P('batch'), may hold values from 0 to 2, never falling along the last dimension, each value on 1 to 2 neighbouring positions
- links: int32 [4, 4], P('batch'), may hold values 0 or 1
Outputs:
- attended: bfloat16 [2048, 4096], P(('batch', 'seq', 'head'))
The draws below stay inside these ranges and needn't reach their ends.
Inputs may be any that keep to these rules, and one draw needn't show every extreme that they name: `page_of_block`: page numbers never fall from one block to the next.
All inputs are finite; a program needn't handle non-finite values.
Results may differ from the reference program's by a relative error of at most 0.0065.
Values may be sent and summed in bfloat16 or wider, within the bound.
No kernel may reach another device: no remote copies, remote signals or barrier semaphores. Data moves between devices by JAX's collectives and lax.ppermute only.
A program may use at most 64 MiB of HBM per device.

```python
import math
import jax
import jax.numpy as jnp
import numpy as np
from jax import lax

QUERY_HEAD_COUNT = 32
KEY_VALUE_HEADS = 4
HEAD_SIZE = 128
BLK = 512
SEQUENCE_TOKENS = 2048
NB = 4


def draw_queries(key, part):
    starting_point = jnp.clip(jax.random.normal(jax.random.fold_in(key, 11), (SEQUENCE_TOKENS, QUERY_HEAD_COUNT, HEAD_SIZE), jnp.float32), -6.0, 6.0)
    return starting_point.reshape(SEQUENCE_TOKENS, QUERY_HEAD_COUNT * HEAD_SIZE).astype(jnp.bfloat16)


def draw_keys(key, part):
    starting_point = jnp.clip(jax.random.normal(jax.random.fold_in(key, 23), (SEQUENCE_TOKENS, KEY_VALUE_HEADS, HEAD_SIZE), jnp.float32), -6.0, 6.0)
    return starting_point.reshape(SEQUENCE_TOKENS, KEY_VALUE_HEADS * HEAD_SIZE).astype(jnp.bfloat16)


def plant(result, key, least, largest):
    longest = result.shape.index(max(result.shape))
    spots = []
    for shift in (0, 1):
        where = [jax.random.randint(jax.random.fold_in(key, axis), (), 0, length) for axis, length in enumerate(result.shape)]
        where[longest] = (where[longest] + shift) % result.shape[longest]
        spots.append(tuple(where))
    return result.at[spots[0]].set(least).at[spots[1]].set(largest)


def levels(rng, dims, cuts, low, top_value):
    factor_of, own = 1.0, jax.random.fold_in(rng, 6)
    for dim, parts in cuts:
        heights = jnp.exp(jax.random.uniform(jax.random.fold_in(own, dim), (parts,), jnp.float32, low / len(cuts), top_value / len(cuts)))
        factor_of = factor_of * jnp.repeat(heights, dims[dim] // parts).reshape([-1 if axis == dim else 1 for axis in range(len(dims))])
    return factor_of


def profile(amount, total, reach, lean):
    weights = [(1 << 20) // math.isqrt(grade ** lean) + 1 for grade in range(2, amount + 1)]
    surplus, counts = total - reach - (amount - 1), [1] * (amount - 1)
    while surplus > 0:
        free = [i for i in range(amount - 1) if counts[i] < reach]
        mass, left = sum([weights[i] for i in free]), surplus
        for i in free:
            addition = min(reach - counts[i], max(1, left * weights[i] // mass), surplus)
            counts[i] = counts[i] + addition
            surplus = surplus - addition
    return np.array([reach] + counts)


def uneven(stream_key, count, total, bound, lean):
    if count == 2:
        one = jax.random.randint(stream_key, (), max(1, total - bound), min(bound, total - 1) + 1)
        return jnp.stack([one, total - one])
    tallies = jnp.asarray(profile(count, total, bound, lean), jnp.int32)
    pairs = (count - 1) // 2
    giver, sink = tallies[1:1 + 2 * pairs:2], tallies[2:2 + 2 * pairs:2]
    room = jnp.minimum(giver - 1, bound - sink)
    shifted = jax.random.randint(jax.random.fold_in(stream_key, 1), (pairs,), 0, 1 << 20) % (room + 1)
    tallies = tallies.at[1:1 + 2 * pairs:2].set(giver - shifted).at[2:2 + 2 * pairs:2].set(sink + shifted)
    return tallies[jax.random.permutation(jax.random.fold_in(stream_key, 2), count)]


def normal_values(rng, dims, scale, reach, cuts=(), kind=jnp.bfloat16):
    drawn = scale * jax.random.normal(rng, dims, jnp.float32)
    if cuts:
        drawn = drawn * levels(rng, dims, cuts, -0.22, 0.18)
    return jnp.clip(drawn, -reach, reach).astype(kind)


def setup_inputs(seed: int = 0, part: int = 0) -> dict:
    streams_of = jax.random.split(jax.random.key(seed), 6)
    part_splits = jax.random.split(jax.random.fold_in(streams_of[5], part), 6)
    queries = draw_queries(jax.random.fold_in(jax.random.fold_in(streams_of[5], part), 71), part)
    keys = draw_keys(jax.random.fold_in(jax.random.fold_in(streams_of[5], part), 71), part)
    values = normal_values(part_splits[2], (SEQUENCE_TOKENS, KEY_VALUE_HEADS * HEAD_SIZE), 1.0, 6.0, ((0, 32),))
    page_of_block = jnp.searchsorted(jnp.cumsum(uneven(part_splits[3], NB // 2 + 1, NB, min(4, NB - NB // 2), 2)), jnp.arange(NB), side="right").astype(jnp.int32)
    links = plant((jax.random.randint(part_splits[4], (NB, NB), 0, 4) < 1).astype(jnp.int32), jax.random.fold_in(part_splits[4], 1), 0, 1)
    return dict(queries=queries, keys=keys, values=values, page_of_block=page_of_block, links=links)


def reference(queries, keys, values, page_of_block, links):
    position = jnp.arange(SEQUENCE_TOKENS, dtype=jnp.int32)
    block_of = position // BLK
    page_ids = page_of_block[block_of]
    same_page = page_ids[:, None] == page_ids[None, :]
    causal = position[None, :] <= position[:, None]
    linked = jnp.repeat(jnp.repeat(links == 1, BLK, axis=0), BLK, axis=1)
    allowed = jnp.where(same_page, causal, linked)
    group_width = QUERY_HEAD_COUNT // KEY_VALUE_HEADS
    query_heads = queries.reshape(SEQUENCE_TOKENS, QUERY_HEAD_COUNT, HEAD_SIZE).transpose(1, 0, 2)
    heads_of_keys = jnp.repeat(keys.reshape(SEQUENCE_TOKENS, KEY_VALUE_HEADS, HEAD_SIZE).transpose(1, 0, 2), group_width, axis=0)
    heads_of_values = jnp.repeat(values.reshape(SEQUENCE_TOKENS, KEY_VALUE_HEADS, HEAD_SIZE).transpose(1, 0, 2), group_width, axis=0)

    def one_head(triple):
        query_head, key_head, value_head = triple
        scores = jnp.dot(query_head, key_head.T, preferred_element_type=jnp.float32) * (HEAD_SIZE ** -0.5)
        scores = jnp.where(allowed, scores, -1e30)
        maximum = jnp.max(scores, axis=1, keepdims=True)
        weights = jnp.where(allowed, jnp.exp(scores - maximum), 0.0)
        totals = jnp.sum(weights, axis=1, keepdims=True)
        mixture = jnp.dot(weights.astype(jnp.bfloat16), value_head, preferred_element_type=jnp.float32)
        return mixture / totals

    attended = lax.map(one_head, (query_heads, heads_of_keys, heads_of_values))
    return attended.transpose(1, 0, 2).reshape(SEQUENCE_TOKENS, QUERY_HEAD_COUNT * HEAD_SIZE).astype(jnp.bfloat16)
```

```python
import math

import jax
import jax.numpy as jnp
from jax import lax
from jax.experimental import pallas as pl
from jax.experimental.pallas import tpu as pltpu
from jax.sharding import PartitionSpec as P

HEAD_SIZE = 128
BLK = 512
AXES = ("seq", "head")


def exchange(array, mask, device_count):
    return lax.ppermute(array, AXES, [(i, i ^ mask) for i in range(device_count)])


def gather_block(piece, bits, device_count):
    arrays = [(piece, (0,))]
    for step, bit in enumerate(bits):
        arrays = arrays + [
            (exchange(array, bit, device_count), tuple(mask ^ bit for mask in masks)) for array, masks in arrays
        ]
        if step == 0 and len(bits) > 1:
            arrays = [
                (
                    jnp.concatenate([array for array, _ in arrays], axis=0),
                    sum((masks for _, masks in arrays), ()),
                )
            ]
    return arrays


def attend_kernel(pages_ref, links_ref, query_ref, *refs, blocks, row_count, kv_count, device_masks):
    piece_refs, (out_ref, max_ref, total_ref, acc_ref) = refs[:-4], refs[-4:]
    kv_width = kv_count * HEAD_SIZE
    group = query_ref.shape[1] // kv_width
    columns = group * row_count
    exp_scale = HEAD_SIZE ** (-0.5) / math.log(2.0)
    here = lax.axis_index(AXES)
    plane = BLK // row_count
    own_block = here // plane
    place = here % plane

    def head_step(head, block, first):
        query = jnp.concatenate(
            [
                query_ref[:, pl.ds(pl.multiple_of((head * group + j) * HEAD_SIZE, HEAD_SIZE), HEAD_SIZE)]
                for j in range(group)
            ],
            axis=0,
        )
        start = pl.multiple_of(head * HEAD_SIZE, HEAD_SIZE)
        value_start = pl.multiple_of(kv_width + head * HEAD_SIZE, HEAD_SIZE)
        keys = jnp.concatenate([piece_refs[i][:, pl.ds(start, HEAD_SIZE)] for i in block], axis=0)
        values = jnp.concatenate([piece_refs[i][:, pl.ds(value_start, HEAD_SIZE)] for i in block], axis=0)
        scores = lax.dot_general(keys, query, (((1,), (1,)), ((), ())), preferred_element_type=jnp.float32)
        if first:
            row = lax.broadcasted_iota(jnp.int32, (row_count, columns), 0)
            query_pos = place * row_count + lax.rem(lax.broadcasted_iota(jnp.int32, (row_count, columns), 1), row_count)
            allowed = jnp.concatenate(
                [row + (place ^ mask) * row_count <= query_pos for i in block for mask in device_masks[i]], axis=0
            )
            scores = jnp.where(allowed, scores, -1e30)
            maximum = jnp.max(scores, axis=0, keepdims=True)
        else:
            previous = max_ref[head]
            maximum = jnp.maximum(previous, jnp.max(scores, axis=0, keepdims=True))
        weights = jnp.exp2(scores * exp_scale - maximum * exp_scale)
        total = jnp.sum(weights, axis=0, keepdims=True)
        product = lax.dot_general(
            values, weights.astype(jnp.bfloat16), (((0,), (0,)), ((), ())), preferred_element_type=jnp.float32
        )
        if not first:
            factor = jnp.exp2((previous - maximum) * exp_scale)
            total = total + total_ref[head] * factor
            product = product + acc_ref[head] * factor
        max_ref[head] = maximum
        total_ref[head] = total
        acc_ref[head] = product

    for order, (block_mask, block) in enumerate(blocks):
        if order == 0:
            pl.loop(0, kv_count)(lambda head, block=block: head_step(head, block, True))
        else:
            other = own_block ^ block_mask
            same = pages_ref[own_block] == pages_ref[other]
            needed = jnp.where(same, other < own_block, links_ref[own_block, other] == 1)

            @pl.when(needed)
            def _(block=block):
                pl.loop(0, kv_count)(lambda head: head_step(head, block, False))

    @pl.loop(0, kv_count)
    def _(head):
        result = (acc_ref[head] / total_ref[head]).T.astype(jnp.bfloat16)
        for j in range(group):
            out_ref[:, pl.ds(pl.multiple_of((head * group + j) * HEAD_SIZE, HEAD_SIZE), HEAD_SIZE)] = result[
                j * row_count : (j + 1) * row_count
            ]


def make_local(device_count):
    def local(queries, keys, values, page_of_block, links):
        row_count = queries.shape[0]
        kv_count = keys.shape[1] // HEAD_SIZE
        group = queries.shape[1] // keys.shape[1]
        plane = BLK // row_count
        block_count = page_of_block.shape[0]
        bits = [plane >> (i + 1) for i in range(plane.bit_length() - 1)]
        own = jnp.concatenate([keys, values], axis=1)
        order = [k for k in range(block_count)]
        blocks, pieces, device_masks = [], [], []
        for turn, k in enumerate(order):
            piece = own if k == 0 else exchange(own, k * plane, device_count)
            here_bits = bits if turn % 2 == 0 or len(bits) < 3 else [bits[1], bits[0]] + bits[2:]
            arrays = gather_block(piece, here_bits, device_count)
            blocks.append((k, tuple(range(len(pieces), len(pieces) + len(arrays)))))
            pieces += [array for array, _ in arrays]
            device_masks += [masks for _, masks in arrays]
        columns = group * row_count

        def body(*refs):
            attend_kernel(
                *refs, blocks=blocks, row_count=row_count, kv_count=kv_count, device_masks=device_masks
            )

        smem = pl.BlockSpec(memory_space=pltpu.SMEM)
        vmem = pl.BlockSpec(memory_space=pltpu.VMEM)
        return pl.pallas_call(
            body,
            name="attend",
            out_shape=jax.ShapeDtypeStruct(queries.shape, queries.dtype),
            in_specs=[smem, smem, vmem] + [vmem] * len(pieces),
            out_specs=vmem,
            scratch_shapes=[
                pltpu.VMEM((kv_count, 1, columns), jnp.float32),
                pltpu.VMEM((kv_count, 1, columns), jnp.float32),
                pltpu.VMEM((kv_count, HEAD_SIZE, columns), jnp.float32),
            ],
            compiler_params=pltpu.CompilerParams(vmem_limit_bytes=48 * 1024 * 1024),
        )(page_of_block, links, queries, *pieces)

    return local


def solution(mesh):
    split = P(("batch", "seq", "head"), None)
    device_count = mesh.shape["seq"] * mesh.shape["head"]
    return jax.shard_map(
        make_local(device_count),
        mesh=mesh,
        in_specs=(split, split, split, P("batch"), P("batch", None)),
        out_specs=split,
        check_vma=False,
    )
```
